512 devices in a mesh: dp: 8 (over z_hi, x), expert: 64 (over y, z_lo, core).
Axes of the slice: x: 4, y: 8, z: 8 (z_hi: 2, z_lo: 4; z = z_hi * 4 + z_lo), core: 2. Of those that a mesh axis runs over, the one named last changes fastest.
Arguments:
- tokens: bfloat16 [65536, 1024], P(('dp', 'expert')), may hold values from -6 to 6
- cotangent: bfloat16 [65536, 1024], P(('dp', 'expert')), may hold values from -6 to 6
- pick_lists: int32 [8, 64, 128], P('dp'), may hold values from 0 to 8191, as said below
- combine: float32 [8, 64, 128], P('dp'), may hold values from 0.1 to 1
- w_gate: bfloat16 [64, 1024, 1024], P('expert', 'dp'), may hold values from -0.1875 to 0.1875
- w_up: bfloat16 [64, 1024, 1024], P('expert', 'dp'), may hold values from -0.1875 to 0.1875
- w_down: bfloat16 [64, 1024, 1024], P('expert', 'dp'), may hold values from -0.1875 to 0.1875
Outputs:
- layer_out: bfloat16 [65536, 1024], P(('dp', 'expert'))
- tokens_grad: bfloat16 [65536, 1024], P(('dp', 'expert'))
- grad_gate: bfloat16 [64, 1024, 1024], P('expert', 'dp')
- grad_up: bfloat16 [64, 1024, 1024], P('expert', 'dp')
- grad_down: bfloat16 [64, 1024, 1024], P('expert', 'dp')
The draws below stay inside these ranges and needn't reach their ends.
Inputs may be any that keep to these rules, and one draw needn't show every extreme that they name: Each list pick_lists[r, e] names 128 distinct tokens of replica r. Token numbers j * 128 to (j + 1) * 128 - 1 are those of the device with index j on the expert axis; at most 4 picks of one expert in one replica fall among one device's tokens, and for every expert and replica exactly 4 fall among some device's.
All inputs are finite; a program needn't handle non-finite values.
Results may differ from the reference program's by a relative error of at most 0.013.
Values may be sent and summed in bfloat16 or wider, within the bound.
No kernel may reach another device: no remote copies, remote signals or barrier semaphores. Data moves between devices by JAX's collectives and lax.ppermute only.
A program may use at most 64 MiB of HBM per device.

```python
import jax
import jax.numpy as jnp
from jax import lax

D = 1024
FF = 1024
TOK_DEV = 128
EXPERTS = 64
CAP = 128
SLOT = 4
TOKENS_REP = 8192
TOKENS = 65536
N_DP = 8
N_EXPERT = 64


def draw_pick_lists(key, part):

    def one_list(list_key):
        key_full, key_order, key_rows, key_shuffle = jax.random.split(list_key, 4)
        full_block = jax.random.randint(key_full, (), 0, N_EXPERT)
        order_ids = jax.random.permutation(key_order, N_EXPERT * SLOT).astype(jnp.int32)
        position = jnp.arange(N_EXPERT * SLOT, dtype=jnp.int32)
        score = jnp.where(position // SLOT == full_block, position - N_EXPERT * SLOT, order_ids)
        taken = jnp.argsort(score, stable=True)[:CAP].astype(jnp.int32)
        block_ids = taken // SLOT
        slot_ids = taken - block_ids * SLOT
        row_tables = jax.vmap(lambda row_key: jax.random.permutation(row_key, TOK_DEV).astype(jnp.int32))(jax.random.split(key_rows, N_EXPERT))
        chosen_rows = row_tables[block_ids, slot_ids]
        chosen = block_ids * TOK_DEV + chosen_rows
        shuffle = jax.random.permutation(key_shuffle, CAP)
        return chosen[shuffle].astype(jnp.int32)
    list_keys = jax.random.split(jax.random.fold_in(key, 17), N_DP * EXPERTS)
    return jax.vmap(one_list)(list_keys).reshape(N_DP, EXPERTS, CAP)


def block_levels(own_key, dims, shards, low, top_value):
    def one(dim, shards_of):
        heights = jax.random.uniform(jax.random.fold_in(jax.random.fold_in(own_key, 6), dim), (shards_of,), jnp.float32, low / len(shards), top_value / len(shards))
        return jnp.repeat(jnp.exp(heights), dims[dim] // shards_of).reshape((-1,) + (1,) * (len(dims) - dim - 1))

    factor_of = one(*shards[0])
    for cut in shards[1:]:
        factor_of = factor_of * one(*cut)
    return factor_of


def noise(stream_key, extent, width, reach, cuts=(), held_as=jnp.bfloat16):
    values = width * jax.random.normal(stream_key, extent, jnp.float32)
    if cuts:
        values = values * block_levels(stream_key, extent, cuts, -0.22, 0.18)
    return jnp.clip(values, -reach, reach).astype(held_as)


def setup_inputs(seed: int = 0) -> dict:
    key_list = jax.random.split(jax.random.key(seed), 8)
    return {
        "tokens": noise(key_list[0], (TOKENS, D), 1.0, 6.0, ((0, 512),)),
        "cotangent": noise(key_list[1], (TOKENS, D), 1.0, 6.0, ((0, 512),)),
        "pick_lists": draw_pick_lists(jax.random.fold_in(key_list[7], 71), 0),
        "combine": jnp.clip(0.1 + 0.9 * jax.random.uniform(key_list[3], (N_DP, EXPERTS, CAP), jnp.float32) ** block_levels(key_list[3], (N_DP, EXPERTS, CAP), ((0, 8),), -0.2, 0.2), 0.1, 1.0),
        "w_gate": noise(key_list[4], (EXPERTS, FF, D), D ** -0.5, 0.1875, ((0, 64), (1, 8))),
        "w_up": noise(key_list[5], (EXPERTS, FF, D), D ** -0.5, 0.1875, ((0, 64), (1, 8))),
        "w_down": noise(key_list[6], (EXPERTS, FF, D), FF ** -0.5, 0.1875, ((0, 64), (1, 8))),
    }


def silu_parts(gate_pre):
    sigma_gate = jax.nn.sigmoid(gate_pre)
    return gate_pre * sigma_gate, sigma_gate


def blocked_sum(left_parts, right_parts):
    parts = jnp.einsum("rbf,bfd->brd", left_parts.astype(jnp.float32), right_parts.astype(jnp.float32))
    parts = parts.astype(jnp.bfloat16)
    parts = lax.optimization_barrier(parts)
    return jnp.sum(parts.astype(jnp.float32), axis=0).astype(jnp.bfloat16)


def reference(tokens, cotangent, pick_lists, combine, w_gate, w_up, w_down):
    tok_rep = tokens.reshape(N_DP, TOKENS_REP, D)
    cot_rep = cotangent.reshape(N_DP, TOKENS_REP, D)
    replica = jnp.arange(N_DP, dtype=jnp.int32)[:, None]
    block_width = FF // N_DP
    rows_all = N_DP * CAP

    def one_expert(inputs):
        chosen_ids, weights, gate_w, up_w, down_w = inputs
        chosen = tok_rep[replica, chosen_ids].reshape(rows_all, D)
        weighted = (weights[:, :, None] * cot_rep[replica, chosen_ids].astype(jnp.float32)).astype(jnp.bfloat16).reshape(rows_all, D)
        gate_pre = jnp.dot(chosen, gate_w.T, preferred_element_type=jnp.float32)
        up_pre = jnp.dot(chosen, up_w.T, preferred_element_type=jnp.float32)
        silu_gate, sigma_gate = silu_parts(gate_pre)
        hidden = (silu_gate * up_pre).astype(jnp.bfloat16)
        expert_out = blocked_sum(hidden.reshape(rows_all, N_DP, block_width), down_w.reshape(N_DP, block_width, D))
        d_hidden = jnp.dot(weighted, down_w.T, preferred_element_type=jnp.float32)
        d_gate = (d_hidden * up_pre * sigma_gate * (1.0 + gate_pre * (1.0 - sigma_gate))).astype(jnp.bfloat16)
        d_up = (d_hidden * silu_gate).astype(jnp.bfloat16)
        gate_parts = jnp.einsum("rbf,bfd->brd", d_gate.reshape(rows_all, N_DP, block_width).astype(jnp.float32), gate_w.reshape(N_DP, block_width, D).astype(jnp.float32))
        up_parts = jnp.einsum("rbf,bfd->brd", d_up.reshape(rows_all, N_DP, block_width).astype(jnp.float32), up_w.reshape(N_DP, block_width, D).astype(jnp.float32))
        back_parts = lax.optimization_barrier((gate_parts + up_parts).astype(jnp.bfloat16))
        d_chosen = jnp.sum(back_parts.astype(jnp.float32), axis=0).astype(jnp.bfloat16)
        grad_gate = jnp.dot(d_gate.T, chosen, preferred_element_type=jnp.float32).astype(jnp.bfloat16)
        grad_up = jnp.dot(d_up.T, chosen, preferred_element_type=jnp.float32).astype(jnp.bfloat16)
        grad_down = jnp.dot(hidden.T, weighted, preferred_element_type=jnp.float32).astype(jnp.bfloat16)
        return expert_out.reshape(N_DP, CAP, D), d_chosen.reshape(N_DP, CAP, D), grad_gate, grad_up, grad_down

    outputs = lax.map(one_expert, (jnp.swapaxes(pick_lists, 0, 1), jnp.swapaxes(combine, 0, 1), w_gate, w_up, w_down))
    expert_out, d_chosen, grad_gate, grad_up, grad_down = outputs
    replica_three = jnp.arange(N_DP, dtype=jnp.int32)[:, None, None]
    out_terms = combine[:, :, :, None] * jnp.swapaxes(expert_out, 0, 1).astype(jnp.float32)
    layer_out = jnp.zeros((N_DP, TOKENS_REP, D), jnp.float32).at[replica_three, pick_lists].add(out_terms)
    back_terms = jnp.swapaxes(d_chosen, 0, 1).astype(jnp.float32)
    tokens_grad = jnp.zeros((N_DP, TOKENS_REP, D), jnp.float32).at[replica_three, pick_lists].add(back_terms)
    layer_out = layer_out.reshape(TOKENS, D).astype(jnp.bfloat16)
    tokens_grad = tokens_grad.reshape(TOKENS, D).astype(jnp.bfloat16)
    return (layer_out, tokens_grad, grad_gate, grad_up, grad_down)
```

```python
import jax
import jax.numpy as jnp
from jax import lax
from jax.experimental import pallas as pl
from jax.experimental.pallas import tpu as pltpu
from jax.sharding import PartitionSpec as P

N_X = 4
N_HALF = 2
SLOT = 4
BF16 = jnp.bfloat16
F32 = jnp.float32

HALF_PAIRS = [[i, i + N_X] for i in range(N_X)]


def x_shift(step):
    return [
        (h * N_X + i, h * N_X + (i + step) % N_X) for h in range(N_HALF) for i in range(N_X)
    ]


def mm(a, b, contract_a, contract_b):
    return lax.dot_general(
        a, b, (((contract_a,), (contract_b,)), ((), ())), preferred_element_type=F32
    )


def kernel_call(body, out_shapes, n_smem, n_vmem, flops, nbytes):
    return pl.pallas_call(
        body,
        out_shape=out_shapes,
        in_specs=[pl.BlockSpec(memory_space=pltpu.SMEM)] * n_smem
        + [pl.BlockSpec(memory_space=pltpu.VMEM)] * n_vmem,
        out_specs=jax.tree.map(lambda _: pl.BlockSpec(memory_space=pltpu.VMEM), out_shapes),
        cost_estimate=pl.CostEstimate(flops=flops, bytes_accessed=nbytes, transcendentals=0),
        compiler_params=pltpu.CompilerParams(vmem_limit_bytes=48 * 1024 * 1024),
    )


def strictly_before(n):
    rows = lax.broadcasted_iota(jnp.int32, (n, n), 0)
    cols = lax.broadcasted_iota(jnp.int32, (n, n), 1)
    return (rows < cols).astype(BF16)


def slot_tables(my, pick, weight, tok_rows):
    n_experts, cap = pick.shape
    low = my * tok_rows
    mine = (pick >= low) & (pick < low + tok_rows)
    rank = mm(mine.astype(F32).astype(BF16), strictly_before(cap), 1, 0)
    code = jnp.where(mine, rank, -1.0)
    place = jnp.where(mine, (pick - low + 1).astype(F32), 0.0)
    shape = (n_experts, 2 * SLOT, cap)
    slot = (lax.broadcasted_iota(jnp.int32, shape, 1) % SLOT).astype(F32)
    hit = jnp.broadcast_to(code[:, None, :], shape) == slot
    row = jnp.sum(
        jnp.where(hit, jnp.broadcast_to(place[:, None, :], shape), 0.0), axis=2, keepdims=True
    )
    share = jnp.sum(
        jnp.where(hit, jnp.broadcast_to(weight[:, None, :], shape), 0.0), axis=2, keepdims=True
    )
    return row - 1.0, share


def send_body(my_ref, pick_ref, weight_ref, tok_ref, cot_ref, out_ref):
    n_experts = pick_ref.shape[0]
    tok_rows = tok_ref.shape[0]
    row, share = slot_tables(my_ref[0], pick_ref[...], weight_ref[...], tok_rows)
    shape = (n_experts, 2 * SLOT, 2 * tok_rows)
    lane = lax.broadcasted_iota(jnp.int32, shape, 2).astype(F32)
    second = lax.broadcasted_iota(jnp.int32, (n_experts, 2 * SLOT, 1), 1) >= SLOT
    target = jnp.where(second & (row >= 0.0), row + float(tok_rows), row)
    scale = jnp.where(second, share, 1.0)
    n_slots = n_experts * 2 * SLOT
    select = (lane == target).astype(F32).reshape(n_slots, 2 * tok_rows).astype(BF16)
    both = jnp.concatenate([tok_ref[...], cot_ref[...]], axis=0)
    rows = mm(select, both, 1, 0)
    scale = jnp.broadcast_to(scale, (n_experts, 2 * SLOT, 128)).reshape(n_slots, 128)
    for c in range(rows.shape[1] // 128):
        part = rows[:, c * 128 : (c + 1) * 128] * scale
        out_ref[:, c * 128 : (c + 1) * 128] = part.astype(BF16)


def table_body(my_ref, pick_ref, weight_ref, place_ref, back_ref):
    n_experts, cap = pick_ref.shape
    my = my_ref[0]
    n_slots = n_experts * 2 * SLOT
    tok_rows = cap_rows = back_ref.shape[1] // 3
    own = pick_ref[pl.ds(my, 1), :]
    source = lax.shift_right_logical(own, 7)
    from_dev = (
        lax.broadcasted_iota(jnp.int32, (n_experts, cap), 0)
        == jnp.broadcast_to(source, (n_experts, cap))
    ).astype(F32)
    rank = jnp.sum(
        from_dev * mm(from_dev.astype(BF16), strictly_before(cap), 1, 0), axis=0, keepdims=True
    )
    position = source * (2 * SLOT) + rank.astype(jnp.int32)
    both = jnp.concatenate([position, position + SLOT], axis=1)
    sub = lax.broadcasted_iota(jnp.int32, (n_slots, 2 * cap), 0)
    place_ref[...] = (sub == jnp.broadcast_to(both, (n_slots, 2 * cap))).astype(F32).astype(BF16)
    row, share = slot_tables(my, pick_ref[...], weight_ref[...], tok_rows)
    shape = (n_experts, 2 * SLOT, tok_rows)
    lane = lax.broadcasted_iota(jnp.int32, shape, 2).astype(F32)
    second = lax.broadcasted_iota(jnp.int32, shape, 1) >= SLOT
    hit = lane == row
    high = share.astype(BF16).astype(F32)
    low = share - high
    zero = jnp.zeros(shape, F32)
    first_hit = hit & ~second
    pieces = (
        jnp.where(first_hit, high, zero),
        jnp.where(hit & second, 1.0, zero),
        jnp.where(first_hit, low, zero),
    )
    for i, piece in enumerate(pieces):
        back_ref[:, i * tok_rows : (i + 1) * tok_rows] = piece.reshape(n_slots, tok_rows).astype(
            BF16
        )


def compact_body(place_ref, recv_ref, chosen_ref, weighted_ref):
    rows = mm(place_ref[...], recv_ref[...], 0, 0).astype(BF16)
    cap = chosen_ref.shape[0]
    chosen_ref[...] = rows[:cap]
    weighted_ref[...] = rows[cap:]


def expert_body(
    half_ref,
    chosen_ref,
    weighted_ref,
    w0,
    w1,
    w2,
    w3,
    own_ref,
    send_out_ref,
    send_back_ref,
    g_own,
    g1,
    g2,
    g3,
):
    half = half_ref[0]
    _, cap, feat = chosen_ref.shape
    chosen = jnp.concatenate([chosen_ref[half], chosen_ref[1 - half]], axis=0)
    weighted = jnp.concatenate([weighted_ref[half], weighted_ref[1 - half]], axis=0)
    width = w0.shape[0] // 3
    out = jnp.zeros((2 * cap, feat), F32)
    back = jnp.zeros((2 * cap, feat), F32)
    for w_ref, g_ref in ((w0, g_own), (w1, g1), (w2, g2), (w3, g3)):
        pre = mm(chosen, w_ref[: 2 * width], 1, 1)
        d_hidden = mm(weighted, w_ref[2 * width :], 1, 1)
        gate, up = pre[:, :width], pre[:, width:]
        sigma = jax.nn.sigmoid(gate)
        silu = gate * sigma
        hidden = (silu * up).astype(BF16)
        d_gate = (d_hidden * up * sigma * (1.0 + gate * (1.0 - sigma))).astype(BF16)
        d_up = (d_hidden * silu).astype(BF16)
        d_both = jnp.concatenate([d_gate, d_up], axis=1)
        out = out + mm(hidden, w_ref[2 * width :], 1, 0)
        back = back + mm(d_both, w_ref[: 2 * width], 1, 0)
        g_ref[: 2 * width] = mm(d_both, chosen, 0, 0).astype(g_ref.dtype)
        g_ref[2 * width :] = mm(hidden, weighted, 0, 0).astype(g_ref.dtype)
    own_ref[:cap] = out[:cap]
    own_ref[cap:] = back[:cap]
    send_out_ref[...] = out[cap:].astype(BF16)
    send_back_ref[...] = back[cap:].astype(BF16)


def expand_body(half_ref, place_ref, own_ref, other_out_ref, other_back_ref, out_ref):
    there = 1 - half_ref[0]
    other = jnp.concatenate([other_out_ref[there], other_back_ref[there]], axis=0)
    total = (own_ref[...] + other.astype(F32)).astype(BF16)
    out_ref[...] = mm(place_ref[...], total, 1, 0).astype(BF16)


def combine_body(back_ref, slots_ref, layer_ref, grad_ref):
    n = layer_ref.shape[0]
    sums = mm(back_ref[...], slots_ref[...], 0, 0)
    layer_ref[...] = (sums[:n] + sums[2 * n :]).astype(BF16)
    grad_ref[...] = sums[n : 2 * n].astype(BF16)


def weight_sum_body(g_own, g1, g2, g3, gate_ref, up_ref, down_ref):
    width = gate_ref.shape[0]
    for i, ref in enumerate((gate_ref, up_ref, down_ref)):
        piece = pl.ds(i * width, width)
        ref[...] = (
            g_own[piece, :]
            + g1[piece, :].astype(F32)
            + g2[piece, :].astype(F32)
            + g3[piece, :].astype(F32)
        ).astype(BF16)


def per_device(tokens, cotangent, pick_lists, combine, w_gate, w_up, w_down):
    n_experts = lax.axis_size("expert")
    tok_rows, feat = tokens.shape
    cap = pick_lists.shape[2]
    width = w_gate.shape[1]
    n_slots = n_experts * 2 * SLOT
    my = lax.axis_index("expert").astype(jnp.int32).reshape(1)
    half = (lax.axis_index("dp") // N_X).astype(jnp.int32).reshape(1)
    sds = jax.ShapeDtypeStruct
    picks, shares = pick_lists[0], combine[0]

    def exchange(rows):
        parts = rows.reshape(n_experts, 2 * SLOT, feat)
        out = lax.all_to_all(parts, "expert", split_axis=0, concat_axis=0, tiled=True)
        return out.reshape(n_slots, feat)

    def pair_gather(rows):
        return lax.all_gather(rows, "dp", axis_index_groups=HALF_PAIRS)

    row_block = sds((cap, feat), BF16)
    send = kernel_call(send_body, sds((n_slots, feat), BF16), 1, 4, 3 * 10**8, 2 * 10**6)(
        my, picks, shares, tokens, cotangent
    )
    recv = exchange(send)
    place, back_table = kernel_call(
        table_body,
        (sds((n_slots, 2 * cap), BF16), sds((n_slots, 3 * tok_rows), BF16)),
        1,
        2,
        10**8,
        10**6,
    )(my, picks, shares)
    w_own = jnp.concatenate([w_gate[0], w_up[0], w_down[0]], axis=0)
    w_others = [lax.ppermute(w_own, "dp", x_shift(s)) for s in (1, -1, 2)]
    chosen, weighted = kernel_call(
        compact_body, (row_block, row_block), 0, 2, 3 * 10**8, 2 * 10**6
    )(place, recv)
    chosen, weighted = pair_gather(chosen), pair_gather(weighted)
    g_shape = (3 * width, feat)
    own_part, send_out, send_back, g_own, *g_others = kernel_call(
        expert_body,
        (sds((2 * cap, feat), F32), row_block, row_block, sds(g_shape, F32))
        + (sds(g_shape, BF16),) * 3,
        1,
        6,
        3 * 10**9,
        10**7,
    )(half, chosen, weighted, w_own, *w_others)
    g_home = [lax.ppermute(g, "dp", x_shift(-s)) for g, s in zip(g_others, (1, -1, 2))]
    other_out, other_back = pair_gather(send_out), pair_gather(send_back)
    slots = kernel_call(expand_body, sds((n_slots, feat), BF16), 1, 4, 3 * 10**8, 4 * 10**6)(
        half, place, own_part, other_out, other_back
    )
    returned = exchange(slots)
    layer_out, tokens_grad = kernel_call(
        combine_body, (sds((tok_rows, feat), BF16),) * 2, 0, 2, 4 * 10**8, 2 * 10**6
    )(back_table, returned)
    grads = kernel_call(
        weight_sum_body, (sds((width, feat), BF16),) * 3, 0, 4, 10**6, 5 * 10**6
    )(g_own, *g_home)
    return (layer_out, tokens_grad) + tuple(g[None] for g in grads)


def solution(mesh):
    rows = P(("dp", "expert"), None)
    lists = P("dp", None, None)
    weights = P("expert", "dp", None)
    return jax.shard_map(
        per_device,
        mesh=mesh,
        in_specs=(rows, rows, lists, lists, weights, weights, weights),
        out_specs=(rows, rows, weights, weights, weights),
        check_vma=False,
    )
```

```python
import jax
import jax.numpy as jnp
from jax import lax
from jax.experimental import pallas as pl
from jax.experimental.pallas import tpu as pltpu
from jax.sharding import PartitionSpec as P

N_X = 4
N_HALF = 2
SLOT = 4
BF16 = jnp.bfloat16
F32 = jnp.float32

HALF_SWAP = [(i, (i + N_X) % (N_X * N_HALF)) for i in range(N_X * N_HALF)]


def x_shift(step):
    return [
        (h * N_X + i, h * N_X + (i + step) % N_X) for h in range(N_HALF) for i in range(N_X)
    ]


def mm(a, b, contract_a, contract_b):
    return lax.dot_general(
        a, b, (((contract_a,), (contract_b,)), ((), ())), preferred_element_type=F32
    )


def kernel_call(body, out_shapes, n_smem, n_vmem, flops, nbytes):
    return pl.pallas_call(
        body,
        out_shape=out_shapes,
        in_specs=[pl.BlockSpec(memory_space=pltpu.SMEM)] * n_smem
        + [pl.BlockSpec(memory_space=pltpu.VMEM)] * n_vmem,
        out_specs=jax.tree.map(lambda _: pl.BlockSpec(memory_space=pltpu.VMEM), out_shapes),
        cost_estimate=pl.CostEstimate(flops=flops, bytes_accessed=nbytes, transcendentals=0),
        compiler_params=pltpu.CompilerParams(vmem_limit_bytes=48 * 1024 * 1024),
    )


def strictly_before(n):
    rows = lax.broadcasted_iota(jnp.int32, (n, n), 0)
    cols = lax.broadcasted_iota(jnp.int32, (n, n), 1)
    return (rows < cols).astype(BF16)


def slot_tables(my, pick, weight, tok_rows):
    n_experts, cap = pick.shape
    low = my * tok_rows
    mine = (pick >= low) & (pick < low + tok_rows)
    rank = mm(mine.astype(F32).astype(BF16), strictly_before(cap), 1, 0)
    code = jnp.where(mine, rank, -1.0)
    place = jnp.where(mine, (pick - low + 1).astype(F32), 0.0)
    shape = (n_experts, 2 * SLOT, cap)
    slot = (lax.broadcasted_iota(jnp.int32, shape, 1) % SLOT).astype(F32)
    hit = jnp.broadcast_to(code[:, None, :], shape) == slot
    row = jnp.sum(
        jnp.where(hit, jnp.broadcast_to(place[:, None, :], shape), 0.0), axis=2, keepdims=True
    )
    share = jnp.sum(
        jnp.where(hit, jnp.broadcast_to(weight[:, None, :], shape), 0.0), axis=2, keepdims=True
    )
    return row - 1.0, share


def send_body(
    my_ref, pick_hbm, weight_hbm, tok_hbm, cot_hbm, out_ref, pick_ref, weight_ref, both_ref, sems
):
    tok_rows = tok_hbm.shape[0]
    copies = [
        pltpu.make_async_copy(pick_hbm, pick_ref, sems.at[0]),
        pltpu.make_async_copy(weight_hbm, weight_ref, sems.at[1]),
        pltpu.make_async_copy(tok_hbm, both_ref.at[:tok_rows], sems.at[2]),
        pltpu.make_async_copy(cot_hbm, both_ref.at[tok_rows:], sems.at[3]),
    ]
    for copy in copies:
        copy.start()
    copies[0].wait()
    copies[1].wait()
    n_experts = pick_ref.shape[0]
    row, share = slot_tables(my_ref[0], pick_ref[...], weight_ref[...], tok_rows)
    shape = (n_experts, 2 * SLOT, 2 * tok_rows)
    lane = lax.broadcasted_iota(jnp.int32, shape, 2).astype(F32)
    second = lax.broadcasted_iota(jnp.int32, (n_experts, 2 * SLOT, 1), 1) >= SLOT
    target = jnp.where(second & (row >= 0.0), row + float(tok_rows), row)
    scale = jnp.where(second, share, 1.0)
    n_slots = n_experts * 2 * SLOT
    select = (lane == target).astype(F32).reshape(n_slots, 2 * tok_rows).astype(BF16)
    scale = jnp.broadcast_to(scale, (n_experts, 2 * SLOT, 128)).reshape(n_slots, 128)
    copies[2].wait()
    copies[3].wait()
    rows = mm(select, both_ref[...], 1, 0)
    for c in range(rows.shape[1] // 128):
        part = rows[:, c * 128 : (c + 1) * 128] * scale
        out_ref[:, c * 128 : (c + 1) * 128] = part.astype(BF16)


def place_body(my_ref, pick_ref, place_ref):
    n_experts, cap = pick_ref.shape
    n_slots = n_experts * 2 * SLOT
    own = pick_ref[pl.ds(my_ref[0], 1), :]
    source = lax.shift_right_logical(own, 7)
    from_dev = (
        lax.broadcasted_iota(jnp.int32, (n_experts, cap), 0)
        == jnp.broadcast_to(source, (n_experts, cap))
    ).astype(F32)
    rank = jnp.sum(
        from_dev * mm(from_dev.astype(BF16), strictly_before(cap), 1, 0), axis=0, keepdims=True
    )
    position = source * (2 * SLOT) + rank.astype(jnp.int32)
    both = jnp.concatenate([position, position + SLOT], axis=1)
    sub = lax.broadcasted_iota(jnp.int32, (n_slots, 2 * cap), 0)
    place_ref[...] = (sub == jnp.broadcast_to(both, (n_slots, 2 * cap))).astype(F32).astype(BF16)


def back_body(my_ref, pick_ref, weight_ref, back_ref):
    n_experts = pick_ref.shape[0]
    n_slots = n_experts * 2 * SLOT
    tok_rows = back_ref.shape[1] // 3
    row, share = slot_tables(my_ref[0], pick_ref[...], weight_ref[...], tok_rows)
    shape = (n_experts, 2 * SLOT, tok_rows)
    lane = lax.broadcasted_iota(jnp.int32, shape, 2).astype(F32)
    second = lax.broadcasted_iota(jnp.int32, shape, 1) >= SLOT
    hit = lane == row
    high = share.astype(BF16).astype(F32)
    low = share - high
    zero = jnp.zeros(shape, F32)
    first_hit = hit & ~second
    pieces = (
        jnp.where(first_hit, high, zero),
        jnp.where(hit & second, 1.0, zero),
        jnp.where(first_hit, low, zero),
    )
    for i, piece in enumerate(pieces):
        back_ref[:, i * tok_rows : (i + 1) * tok_rows] = piece.reshape(n_slots, tok_rows).astype(
            BF16
        )


def compact_body(place_ref, recv_ref, out_ref):
    out_ref[...] = mm(place_ref[...], recv_ref[...], 0, 0).astype(BF16)


def expert_body(rows_ref, w0, w1, w2, w3, part_ref, act_ref):
    cap = rows_ref.shape[0] // 2
    chosen, weighted = rows_ref[:cap], rows_ref[cap:]
    width = w0.shape[0] // 3
    out = jnp.zeros((cap, rows_ref.shape[1]), F32)
    back = jnp.zeros((cap, rows_ref.shape[1]), F32)
    for i, w_ref in enumerate((w0, w1, w2, w3)):
        pre = mm(chosen, w_ref[: 2 * width], 1, 1)
        d_hidden = mm(weighted, w_ref[2 * width :], 1, 1)
        gate, up = pre[:, :width], pre[:, width:]
        sigma = jax.nn.sigmoid(gate)
        silu = gate * sigma
        hidden = (silu * up).astype(BF16)
        d_gate = (d_hidden * up * sigma * (1.0 + gate * (1.0 - sigma))).astype(BF16)
        d_up = (d_hidden * silu).astype(BF16)
        d_both = jnp.concatenate([d_gate, d_up], axis=1)
        out = out + mm(hidden, w_ref[2 * width :], 1, 0)
        back = back + mm(d_both, w_ref[: 2 * width], 1, 0)
        act_ref[i, :, : 2 * width] = d_both
        act_ref[i, :, 2 * width :] = hidden
    part_ref[:cap] = out.astype(part_ref.dtype)
    part_ref[cap:] = back.astype(part_ref.dtype)


def grads_body(rows_here, rows_there, act_here, act_there, g_own, g1, g2, g3):
    cap = rows_here.shape[0] // 2
    width = g_own.shape[0] // 3
    chosen = jnp.concatenate([rows_here[:cap], rows_there[:cap]], axis=0)
    weighted = jnp.concatenate([rows_here[cap:], rows_there[cap:]], axis=0)
    for i, g_ref in ((3, g3), (1, g1), (2, g2), (0, g_own)):
        act = jnp.concatenate([act_here[i], act_there[i]], axis=0)
        g_ref[: 2 * width] = mm(act[:, : 2 * width], chosen, 0, 0).astype(g_ref.dtype)
        g_ref[2 * width :] = mm(act[:, 2 * width :], weighted, 0, 0).astype(g_ref.dtype)


def expand_body(place_ref, own_ref, other_ref, out_ref):
    total = (own_ref[...] + other_ref[...].astype(F32)).astype(BF16)
    out_ref[...] = mm(place_ref[...], total, 1, 0).astype(BF16)


def combine_body(back_ref, slots_ref, layer_ref, grad_ref):
    n = layer_ref.shape[0]
    sums = mm(back_ref[...], slots_ref[...], 0, 0)
    layer_ref[...] = (sums[:n] + sums[2 * n :]).astype(BF16)
    grad_ref[...] = sums[n : 2 * n].astype(BF16)


def weight_sum_body(g_own, g1, g2, g3, gate_ref, up_ref, down_ref):
    width = gate_ref.shape[0]
    for i, ref in enumerate((gate_ref, up_ref, down_ref)):
        piece = pl.ds(i * width, width)
        ref[...] = (
            g_own[piece, :]
            + g1[piece, :].astype(F32)
            + g2[piece, :].astype(F32)
            + g3[piece, :].astype(F32)
        ).astype(BF16)


def per_device(tokens, cotangent, pick_lists, combine, w_gate, w_up, w_down):
    n_experts = lax.axis_size("expert")
    tok_rows, feat = tokens.shape
    cap = pick_lists.shape[2]
    width = w_gate.shape[1]
    n_slots = n_experts * 2 * SLOT
    my = lax.axis_index("expert").astype(jnp.int32).reshape(1)
    sds = jax.ShapeDtypeStruct
    picks, shares = pick_lists[0], combine[0]
    row_pair = sds((2 * cap, feat), BF16)
    slot_rows = sds((n_slots, feat), BF16)

    def exchange(rows):
        parts = rows.reshape(n_experts, 2 * SLOT, feat)
        out = lax.all_to_all(parts, "expert", split_axis=0, concat_axis=0, tiled=True)
        return out.reshape(n_slots, feat)

    hbm = pl.BlockSpec(memory_space=pl.ANY)
    send = pl.pallas_call(
        send_body,
        out_shape=slot_rows,
        in_specs=[pl.BlockSpec(memory_space=pltpu.SMEM)] + [hbm] * 4,
        out_specs=pl.BlockSpec(memory_space=pltpu.VMEM),
        scratch_shapes=[
            pltpu.VMEM(picks.shape, picks.dtype),
            pltpu.VMEM(shares.shape, shares.dtype),
            pltpu.VMEM((2 * tok_rows, feat), BF16),
            pltpu.SemaphoreType.DMA((4,)),
        ],
        cost_estimate=pl.CostEstimate(flops=3 * 10**8, bytes_accessed=2 * 10**6, transcendentals=0),
    )(my, picks, shares, tokens, cotangent)
    recv = exchange(send)
    place = kernel_call(place_body, sds((n_slots, 2 * cap), BF16), 1, 1, 10**7, 10**6)(my, picks)
    w_own = jnp.concatenate([w_gate[0], w_up[0], w_down[0]], axis=0)
    w_all = [w_own] + [lax.ppermute(w_own, "dp", x_shift(s)) for s in (1, -1, 2)]
    rows = kernel_call(compact_body, row_pair, 0, 2, 3 * 10**8, 2 * 10**6)(place, recv)
    rows_there = lax.ppermute(rows, "dp", HALF_SWAP)
    act = sds((len(w_all), cap, 3 * width), BF16)

    def expert(rows_of_one, part):
        return kernel_call(expert_body, (part, act), 0, 5, 10**9, 7 * 10**6)(rows_of_one, *w_all)

    part_here, act_here = expert(rows, sds(row_pair.shape, F32))
    part_there, act_there = expert(rows_there, row_pair)
    part_back = lax.ppermute(part_there, "dp", HALF_SWAP)
    g_shape = (3 * width, feat)
    g_own, *g_others = kernel_call(
        grads_body, (sds(g_shape, F32),) + (sds(g_shape, BF16),) * 3, 0, 4, 10**9, 6 * 10**6
    )(rows, rows_there, act_here, act_there)
    g_home = [lax.ppermute(g, "dp", x_shift(-s)) for g, s in zip(g_others, (1, -1, 2))]
    slots = kernel_call(expand_body, slot_rows, 0, 3, 3 * 10**8, 4 * 10**6)(
        place, part_here, part_back
    )
    returned = exchange(slots)
    back_table = kernel_call(
        back_body, sds((n_slots, 3 * tok_rows), BF16), 1, 2, 10**7, 10**6
    )(my, picks, shares)
    layer_out, tokens_grad = kernel_call(
        combine_body, (sds((tok_rows, feat), BF16),) * 2, 0, 2, 4 * 10**8, 2 * 10**6
    )(back_table, returned)
    grads = kernel_call(
        weight_sum_body, (sds((width, feat), BF16),) * 3, 0, 4, 10**6, 5 * 10**6
    )(g_own, *g_home)
    return (layer_out, tokens_grad) + tuple(g[None] for g in grads)


def solution(mesh):
    rows = P(("dp", "expert"), None)
    lists = P("dp", None, None)
    weights = P("expert", "dp", None)
    return jax.shard_map(
        per_device,
        mesh=mesh,
        in_specs=(rows, rows, lists, lists, weights, weights, weights),
        out_specs=(rows, rows, weights, weights, weights),
        check_vma=False,
    )
```

```python
import functools

import jax
import jax.numpy as jnp
from jax import lax
from jax.experimental import pallas as pl
from jax.experimental.pallas import tpu as pltpu
from jax.sharding import PartitionSpec as P

N_X = 4
N_HALF = 2
CHUNKS = 2
SLOT = 4
BF16 = jnp.bfloat16
F32 = jnp.float32

HALF_SWAP = [(i, (i + N_X) % (N_X * N_HALF)) for i in range(N_X * N_HALF)]


def x_shift(step):
    return [
        (h * N_X + i, h * N_X + (i + step) % N_X) for h in range(N_HALF) for i in range(N_X)
    ]


def mm(a, b, contract_a, contract_b):
    return lax.dot_general(
        a, b, (((contract_a,), (contract_b,)), ((), ())), preferred_element_type=F32
    )


def kernel_call(body, out_shapes, n_smem, n_vmem, flops, nbytes):
    return pl.pallas_call(
        body,
        out_shape=out_shapes,
        in_specs=[pl.BlockSpec(memory_space=pltpu.SMEM)] * n_smem
        + [pl.BlockSpec(memory_space=pltpu.VMEM)] * n_vmem,
        out_specs=jax.tree.map(lambda _: pl.BlockSpec(memory_space=pltpu.VMEM), out_shapes),
        cost_estimate=pl.CostEstimate(flops=flops, bytes_accessed=nbytes, transcendentals=0),
        compiler_params=pltpu.CompilerParams(vmem_limit_bytes=24 * 1024 * 1024),
    )


def strictly_before(n):
    rows = lax.broadcasted_iota(jnp.int32, (n, n), 0)
    cols = lax.broadcasted_iota(jnp.int32, (n, n), 1)
    return (rows < cols).astype(BF16)


def slot_tables(my, pick, weight, tok_rows):
    n_experts, cap = pick.shape
    low = my * tok_rows
    mine = (pick >= low) & (pick < low + tok_rows)
    rank = mm(mine.astype(F32).astype(BF16), strictly_before(cap), 1, 0)
    code = jnp.where(mine, rank, -1.0)
    place = jnp.where(mine, (pick - low + 1).astype(F32), 0.0)
    shape = (n_experts, 2 * SLOT, cap)
    slot = (lax.broadcasted_iota(jnp.int32, shape, 1) % SLOT).astype(F32)
    hit = jnp.broadcast_to(code[:, None, :], shape) == slot
    row = jnp.sum(
        jnp.where(hit, jnp.broadcast_to(place[:, None, :], shape), 0.0), axis=2, keepdims=True
    )
    share = jnp.sum(
        jnp.where(hit, jnp.broadcast_to(weight[:, None, :], shape), 0.0), axis=2, keepdims=True
    )
    return row - 1.0, share


def send_body(
    my_ref, pick_hbm, weight_hbm, tok_hbm, cot_hbm, out_ref, pick_ref, weight_ref, both_ref, sems
):
    tok_rows = tok_hbm.shape[0]
    copies = [
        pltpu.make_async_copy(pick_hbm, pick_ref, sems.at[0]),
        pltpu.make_async_copy(weight_hbm, weight_ref, sems.at[1]),
        pltpu.make_async_copy(tok_hbm, both_ref.at[:tok_rows], sems.at[2]),
        pltpu.make_async_copy(cot_hbm, both_ref.at[tok_rows:], sems.at[3]),
    ]
    for copy in copies:
        copy.start()
    copies[0].wait()
    copies[1].wait()
    n_experts = pick_ref.shape[0]
    row, share = slot_tables(my_ref[0], pick_ref[...], weight_ref[...], tok_rows)
    shape = (n_experts, 2 * SLOT, 2 * tok_rows)
    lane = lax.broadcasted_iota(jnp.int32, shape, 2).astype(F32)
    second = lax.broadcasted_iota(jnp.int32, (n_experts, 2 * SLOT, 1), 1) >= SLOT
    target = jnp.where(second & (row >= 0.0), row + float(tok_rows), row)
    scale = jnp.where(second, share, 1.0)
    n_slots = n_experts * 2 * SLOT
    select = (lane == target).astype(F32).reshape(n_slots, 2 * tok_rows).astype(BF16)
    scale = jnp.broadcast_to(scale, (n_experts, 2 * SLOT, 128)).reshape(n_slots, 128)
    copies[2].wait()
    copies[3].wait()
    rows = mm(select, both_ref[...], 1, 0)
    for c in range(rows.shape[1] // 128):
        part = rows[:, c * 128 : (c + 1) * 128] * scale
        out_ref[:, c * 128 : (c + 1) * 128] = part.astype(BF16)


def place_body(my_ref, pick_ref, place_ref):
    n_experts, cap = pick_ref.shape
    n_slots = n_experts * 2 * SLOT
    own = pick_ref[pl.ds(my_ref[0], 1), :]
    source = lax.shift_right_logical(own, 7)
    from_dev = (
        lax.broadcasted_iota(jnp.int32, (n_experts, cap), 0)
        == jnp.broadcast_to(source, (n_experts, cap))
    ).astype(F32)
    rank = jnp.sum(
        from_dev * mm(from_dev.astype(BF16), strictly_before(cap), 1, 0), axis=0, keepdims=True
    )
    position = source * (2 * SLOT) + rank.astype(jnp.int32)
    both = jnp.concatenate([position, position + SLOT], axis=1)
    sub = lax.broadcasted_iota(jnp.int32, (n_slots, 2 * cap), 0)
    place_ref[...] = (sub == jnp.broadcast_to(both, (n_slots, 2 * cap))).astype(F32).astype(BF16)


def back_body(my_ref, pick_ref, weight_ref, back_ref):
    n_experts = pick_ref.shape[0]
    n_slots = n_experts * 2 * SLOT
    tok_rows = back_ref.shape[1] // 3
    row, share = slot_tables(my_ref[0], pick_ref[...], weight_ref[...], tok_rows)
    shape = (n_experts, 2 * SLOT, tok_rows)
    lane = lax.broadcasted_iota(jnp.int32, shape, 2).astype(F32)
    second = lax.broadcasted_iota(jnp.int32, shape, 1) >= SLOT
    hit = lane == row
    high = share.astype(BF16).astype(F32)
    low = share - high
    zero = jnp.zeros(shape, F32)
    first_hit = hit & ~second
    pieces = (
        jnp.where(first_hit, high, zero),
        jnp.where(hit & second, 1.0, zero),
        jnp.where(first_hit, low, zero),
    )
    for i, piece in enumerate(pieces):
        back_ref[:, i * tok_rows : (i + 1) * tok_rows] = piece.reshape(n_slots, tok_rows).astype(
            BF16
        )


def chunk_rows(refs):
    n = refs[0].shape[0] // 2
    return (
        jnp.concatenate([ref[:n] for ref in refs], axis=0),
        jnp.concatenate([ref[n:] for ref in refs], axis=0),
    )


def compact_body(place_ref, recv_ref, *chunk_refs):
    rows = mm(place_ref[...], recv_ref[...], 0, 0).astype(BF16)
    n = chunk_refs[0].shape[0] // 2
    for c, ref in enumerate(chunk_refs):
        ref[:n] = rows[c * n : (c + 1) * n]
        ref[n:] = rows[(c + len(chunk_refs)) * n : (c + len(chunk_refs) + 1) * n]


def expert_body(n_chunks, *refs):
    chunks, w_refs, (part_ref, act_ref) = refs[:n_chunks], refs[n_chunks:-2], refs[-2:]
    chosen, weighted = chunk_rows(chunks)
    n = chosen.shape[0]
    width = w_refs[0].shape[0] // 3
    out = jnp.zeros(chosen.shape, F32)
    back = jnp.zeros(chosen.shape, F32)
    for i, w_ref in enumerate(w_refs):
        pre = mm(chosen, w_ref[: 2 * width], 1, 1)
        d_hidden = mm(weighted, w_ref[2 * width :], 1, 1)
        gate, up = pre[:, :width], pre[:, width:]
        sigma = jax.nn.sigmoid(gate)
        silu = gate * sigma
        hidden = (silu * up).astype(BF16)
        d_gate = (d_hidden * up * sigma * (1.0 + gate * (1.0 - sigma))).astype(BF16)
        d_up = (d_hidden * silu).astype(BF16)
        d_both = jnp.concatenate([d_gate, d_up], axis=1)
        out = out + mm(hidden, w_ref[2 * width :], 1, 0)
        back = back + mm(d_both, w_ref[: 2 * width], 1, 0)
        act_ref[i, :, : 2 * width] = d_both
        act_ref[i, :, 2 * width :] = hidden
    part_ref[:n] = out.astype(part_ref.dtype)
    part_ref[n:] = back.astype(part_ref.dtype)


def grads_body(n_chunks, *refs):
    chunks = refs[: 2 * n_chunks]
    acts = refs[2 * n_chunks : 3 * n_chunks + 1]
    g_own, g1, g2, g3 = refs[3 * n_chunks + 1 :]
    width = g_own.shape[0] // 3
    chosen, weighted = chunk_rows(chunks)
    for i, g_ref in ((3, g3), (1, g1), (2, g2), (0, g_own)):
        act = jnp.concatenate([ref[i] for ref in acts], axis=0)
        g_ref[: 2 * width] = mm(act[:, : 2 * width], chosen, 0, 0).astype(g_ref.dtype)
        g_ref[2 * width :] = mm(act[:, 2 * width :], weighted, 0, 0).astype(g_ref.dtype)


def expand_body(place_ref, own_ref, *refs):
    other = jnp.concatenate(chunk_rows(refs[:-1]), axis=0)
    total = (own_ref[...] + other.astype(F32)).astype(BF16)
    refs[-1][...] = mm(place_ref[...], total, 1, 0).astype(BF16)


def combine_body(back_ref, slots_ref, layer_ref, grad_ref):
    n = layer_ref.shape[0]
    sums = mm(back_ref[...], slots_ref[...], 0, 0)
    layer_ref[...] = (sums[:n] + sums[2 * n :]).astype(BF16)
    grad_ref[...] = sums[n : 2 * n].astype(BF16)


def weight_sum_body(g_own, g1, g2, g3, gate_ref, up_ref, down_ref):
    width = gate_ref.shape[0]
    for i, ref in enumerate((gate_ref, up_ref, down_ref)):
        piece = pl.ds(i * width, width)
        ref[...] = (
            g_own[piece, :]
            + g1[piece, :].astype(F32)
            + g2[piece, :].astype(F32)
            + g3[piece, :].astype(F32)
        ).astype(BF16)


def per_device(tokens, cotangent, pick_lists, combine, w_gate, w_up, w_down):
    n_experts = lax.axis_size("expert")
    tok_rows, feat = tokens.shape
    cap = pick_lists.shape[2]
    width = w_gate.shape[1]
    n_slots = n_experts * 2 * SLOT
    my = lax.axis_index("expert").astype(jnp.int32).reshape(1)
    sds = jax.ShapeDtypeStruct
    picks, shares = pick_lists[0], combine[0]
    slot_rows = sds((n_slots, feat), BF16)

    def exchange(rows):
        parts = rows.reshape(n_experts, 2 * SLOT, feat)
        out = lax.all_to_all(parts, "expert", split_axis=0, concat_axis=0, tiled=True)
        return out.reshape(n_slots, feat)

    hbm = pl.BlockSpec(memory_space=pl.ANY)
    send = pl.pallas_call(
        send_body,
        out_shape=slot_rows,
        in_specs=[pl.BlockSpec(memory_space=pltpu.SMEM)] + [hbm] * 4,
        out_specs=pl.BlockSpec(memory_space=pltpu.VMEM),
        scratch_shapes=[
            pltpu.VMEM(picks.shape, picks.dtype),
            pltpu.VMEM(shares.shape, shares.dtype),
            pltpu.VMEM((2 * tok_rows, feat), BF16),
            pltpu.SemaphoreType.DMA((4,)),
        ],
        cost_estimate=pl.CostEstimate(flops=3 * 10**8, bytes_accessed=2 * 10**6, transcendentals=0),
    )(my, picks, shares, tokens, cotangent)
    recv = exchange(send)
    place = kernel_call(place_body, sds((n_slots, 2 * cap), BF16), 1, 1, 10**7, 10**6)(my, picks)
    w_own = jnp.concatenate([w_gate[0], w_up[0], w_down[0]], axis=0)
    w_all = [w_own] + [lax.ppermute(w_own, "dp", x_shift(s)) for s in (1, -1, 2)]
    chunk = sds((2 * cap // CHUNKS, feat), BF16)
    rows = kernel_call(compact_body, (chunk,) * CHUNKS, 0, 2, 3 * 10**8, 2 * 10**6)(
        place, recv
    )

    def expert(chunks, dtype):
        n_rows = sum(c.shape[0] for c in chunks)
        outs = (sds((n_rows, feat), dtype), sds((len(w_all), n_rows // 2, 3 * width), BF16))
        body = functools.partial(expert_body, len(chunks))
        n_in = len(chunks) + len(w_all)
        return kernel_call(body, outs, 0, n_in, 10**9, 6 * 10**6)(*chunks, *w_all)

    rows_there, acts_there, parts_back = [], [], []
    for c in range(CHUNKS):
        rows_there.append(lax.ppermute(rows[c], "dp", HALF_SWAP))
    part_here, act_here = expert(rows, F32)
    for c in range(CHUNKS):
        part_there, act_there = expert(rows_there[c : c + 1], BF16)
        acts_there.append(act_there)
        parts_back.append(lax.ppermute(part_there, "dp", HALF_SWAP))
    g_shape = (3 * width, feat)
    g_own, *g_others = kernel_call(
        functools.partial(grads_body, CHUNKS),
        (sds(g_shape, F32),) + (sds(g_shape, BF16),) * 3,
        0,
        3 * CHUNKS + 1,
        10**9,
        6 * 10**6,
    )(*rows, *rows_there, act_here, *acts_there)
    g_home = [lax.ppermute(g, "dp", x_shift(-s)) for g, s in zip(g_others, (1, -1, 2))]
    slots = kernel_call(expand_body, slot_rows, 0, 2 + CHUNKS, 3 * 10**8, 4 * 10**6)(
        place, part_here, *parts_back
    )
    returned = exchange(slots)
    back_table = kernel_call(
        back_body, sds((n_slots, 3 * tok_rows), BF16), 1, 2, 10**7, 10**6
    )(my, picks, shares)
    layer_out, tokens_grad = kernel_call(
        combine_body, (sds((tok_rows, feat), BF16),) * 2, 0, 2, 4 * 10**8, 2 * 10**6
    )(back_table, returned)
    grads = kernel_call(
        weight_sum_body, (sds((width, feat), BF16),) * 3, 0, 4, 10**6, 5 * 10**6
    )(g_own, *g_home)
    return (layer_out, tokens_grad) + tuple(g[None] for g in grads)


def solution(mesh):
    rows = P(("dp", "expert"), None)
    lists = P("dp", None, None)
    weights = P("expert", "dp", None)
    return jax.shard_map(
        per_device,
        mesh=mesh,
        in_specs=(rows, rows, lists, lists, weights, weights, weights),
        out_specs=(rows, rows, weights, weights, weights),
        check_vma=False,
    )
```

```python
import jax
import jax.numpy as jnp
from jax import lax
from jax.experimental import pallas as pl
from jax.experimental.pallas import tpu as pltpu
from jax.sharding import PartitionSpec as P

N_X = 4
N_HALF = 2
SLOT = 4
BF16 = jnp.bfloat16
F32 = jnp.float32

HALF_SWAP = [(i, (i + N_X) % (N_X * N_HALF)) for i in range(N_X * N_HALF)]


def x_shift(step):
    return [
        (h * N_X + i, h * N_X + (i + step) % N_X) for h in range(N_HALF) for i in range(N_X)
    ]


def mm(a, b, contract_a, contract_b):
    return lax.dot_general(
        a, b, (((contract_a,), (contract_b,)), ((), ())), preferred_element_type=F32
    )


def kernel_call(body, out_shapes, n_smem, n_vmem, flops, nbytes):
    return pl.pallas_call(
        body,
        out_shape=out_shapes,
        in_specs=[pl.BlockSpec(memory_space=pltpu.SMEM)] * n_smem
        + [pl.BlockSpec(memory_space=pltpu.VMEM)] * n_vmem,
        out_specs=jax.tree.map(lambda _: pl.BlockSpec(memory_space=pltpu.VMEM), out_shapes),
        cost_estimate=pl.CostEstimate(flops=flops, bytes_accessed=nbytes, transcendentals=0),
        compiler_params=pltpu.CompilerParams(vmem_limit_bytes=24 * 1024 * 1024),
    )


def strictly_before(n):
    rows = lax.broadcasted_iota(jnp.int32, (n, n), 0)
    cols = lax.broadcasted_iota(jnp.int32, (n, n), 1)
    return (rows < cols).astype(BF16)


def slot_tables(my, pick, weight, tok_rows):
    n_experts, cap = pick.shape
    low = my * tok_rows
    mine = (pick >= low) & (pick < low + tok_rows)
    rank = mm(mine.astype(F32).astype(BF16), strictly_before(cap), 1, 0)
    code = jnp.where(mine, rank, -1.0)
    place = jnp.where(mine, (pick - low + 1).astype(F32), 0.0)
    shape = (n_experts, 2 * SLOT, cap)
    slot = (lax.broadcasted_iota(jnp.int32, shape, 1) % SLOT).astype(F32)
    hit = jnp.broadcast_to(code[:, None, :], shape) == slot
    row = jnp.sum(
        jnp.where(hit, jnp.broadcast_to(place[:, None, :], shape), 0.0), axis=2, keepdims=True
    )
    share = jnp.sum(
        jnp.where(hit, jnp.broadcast_to(weight[:, None, :], shape), 0.0), axis=2, keepdims=True
    )
    return row - 1.0, share


def send_body(
    my_ref, pick_hbm, weight_hbm, tok_hbm, cot_hbm, out_ref, pick_ref, weight_ref, both_ref, sems
):
    tok_rows = tok_hbm.shape[0]
    copies = [
        pltpu.make_async_copy(pick_hbm, pick_ref, sems.at[0]),
        pltpu.make_async_copy(weight_hbm, weight_ref, sems.at[1]),
        pltpu.make_async_copy(tok_hbm, both_ref.at[:tok_rows], sems.at[2]),
        pltpu.make_async_copy(cot_hbm, both_ref.at[tok_rows:], sems.at[3]),
    ]
    for copy in copies:
        copy.start()
    copies[0].wait()
    copies[1].wait()
    n_experts = pick_ref.shape[0]
    row, share = slot_tables(my_ref[0], pick_ref[...], weight_ref[...], tok_rows)
    shape = (n_experts, 2 * SLOT, 2 * tok_rows)
    lane = lax.broadcasted_iota(jnp.int32, shape, 2).astype(F32)
    second = lax.broadcasted_iota(jnp.int32, (n_experts, 2 * SLOT, 1), 1) >= SLOT
    target = jnp.where(second & (row >= 0.0), row + float(tok_rows), row)
    scale = jnp.where(second, share, 1.0)
    n_slots = n_experts * 2 * SLOT
    select = (lane == target).astype(F32).reshape(n_slots, 2 * tok_rows).astype(BF16)
    scale = jnp.broadcast_to(scale, (n_experts, 2 * SLOT, 128)).reshape(n_slots, 128)
    copies[2].wait()
    copies[3].wait()
    rows = mm(select, both_ref[...], 1, 0)
    for c in range(rows.shape[1] // 128):
        part = rows[:, c * 128 : (c + 1) * 128] * scale
        out_ref[:, c * 128 : (c + 1) * 128] = part.astype(BF16)


def place_table(my, pick_ref):
    n_experts, cap = pick_ref.shape
    n_slots = n_experts * 2 * SLOT
    own = pick_ref[pl.ds(my, 1), :]
    source = lax.shift_right_logical(own, 7)
    from_dev = (
        lax.broadcasted_iota(jnp.int32, (n_experts, cap), 0)
        == jnp.broadcast_to(source, (n_experts, cap))
    ).astype(F32)
    rank = jnp.sum(
        from_dev * mm(from_dev.astype(BF16), strictly_before(cap), 1, 0), axis=0, keepdims=True
    )
    position = source * (2 * SLOT) + rank.astype(jnp.int32)
    both = jnp.concatenate([position, position + SLOT], axis=1)
    sub = lax.broadcasted_iota(jnp.int32, (n_slots, 2 * cap), 0)
    return (sub == jnp.broadcast_to(both, (n_slots, 2 * cap))).astype(F32).astype(BF16)


def combine_body(my_ref, pick_ref, weight_ref, slots_ref, layer_ref, grad_ref):
    n_experts = pick_ref.shape[0]
    tok_rows = layer_ref.shape[0]
    n_slots = n_experts * 2 * SLOT
    row, share = slot_tables(my_ref[0], pick_ref[...], weight_ref[...], tok_rows)
    shape = (n_experts, 2 * SLOT, tok_rows)
    lane = lax.broadcasted_iota(jnp.int32, shape, 2).astype(F32)
    second = lax.broadcasted_iota(jnp.int32, shape, 1) >= SLOT
    hit = lane == row
    high = share.astype(BF16).astype(F32)
    low = share - high
    zero = jnp.zeros(shape, F32)
    first_hit = hit & ~second
    pieces = (
        jnp.where(first_hit, high, zero),
        jnp.where(hit & second, 1.0, zero),
        jnp.where(first_hit, low, zero),
    )
    table = jnp.concatenate([p.reshape(n_slots, tok_rows).astype(BF16) for p in pieces], axis=1)
    sums = mm(table, slots_ref[...], 0, 0)
    layer_ref[...] = (sums[:tok_rows] + sums[2 * tok_rows :]).astype(BF16)
    grad_ref[...] = sums[tok_rows : 2 * tok_rows].astype(BF16)


def compact_body(my_ref, pick_ref, recv_ref, chosen_ref, weighted_ref):
    rows = mm(place_table(my_ref[0], pick_ref), recv_ref[...], 0, 0).astype(BF16)
    cap = chosen_ref.shape[0]
    chosen_ref[...] = rows[:cap]
    weighted_ref[...] = rows[cap:]


def forward(chosen, w_ref):
    width = w_ref.shape[0] // 3
    pre = mm(chosen, w_ref[: 2 * width], 1, 1)
    gate, up = pre[:, :width], pre[:, width:]
    sigma = jax.nn.sigmoid(gate)
    silu = gate * sigma
    slope = up * sigma * (1.0 + gate * (1.0 - sigma))
    return (silu * up).astype(BF16), slope, silu


def backward(weighted, slope, silu, w_ref):
    d_hidden = mm(weighted, w_ref[2 * (w_ref.shape[0] // 3) :], 1, 1)
    return jnp.concatenate([(d_hidden * slope).astype(BF16), (d_hidden * silu).astype(BF16)], axis=1)


def forward_body(chosen_ref, w0, w1, w2, w3, out_ref, hidden_ref, factor_ref):
    width = w0.shape[0] // 3
    chosen = chosen_ref[...]
    out = jnp.zeros(chosen.shape, F32)
    for i, w_ref in enumerate((w0, w1, w2, w3)):
        hidden, slope, silu = forward(chosen, w_ref)
        out = out + mm(hidden, w_ref[2 * width :], 1, 0)
        hidden_ref[i] = hidden
        factor_ref[i, :, :width] = slope
        factor_ref[i, :, width:] = silu
    out_ref[...] = out.astype(BF16)


def backward_body(weighted_ref, factor_ref, w0, w1, w2, w3, back_ref, d_ref):
    width = w0.shape[0] // 3
    weighted = weighted_ref[...]
    back = jnp.zeros(weighted.shape, F32)
    for i, w_ref in enumerate((w0, w1, w2, w3)):
        d_both = backward(weighted, factor_ref[i, :, :width], factor_ref[i, :, width:], w_ref)
        back = back + mm(d_both, w_ref[: 2 * width], 1, 0)
        d_ref[i] = d_both
    back_ref[...] = back.astype(BF16)


def here_body(chosen_ref, weighted_ref, w0, w1, w2, w3, part_ref, hidden_ref, d_ref):
    width = w0.shape[0] // 3
    chosen, weighted = chosen_ref[...], weighted_ref[...]
    cap = chosen.shape[0]
    out = jnp.zeros(chosen.shape, F32)
    back = jnp.zeros(chosen.shape, F32)
    for i, w_ref in enumerate((w0, w1, w2, w3)):
        hidden, slope, silu = forward(chosen, w_ref)
        d_both = backward(weighted, slope, silu, w_ref)
        out = out + mm(hidden, w_ref[2 * width :], 1, 0)
        back = back + mm(d_both, w_ref[: 2 * width], 1, 0)
        hidden_ref[i] = hidden
        d_ref[i] = d_both
    part_ref[:cap] = out
    part_ref[cap:] = back


def grads_body(blocks, chosen2, weighted2, hidden2, d2, *g_refs):
    chosen = jnp.concatenate([ref[...] for ref in chosen2], axis=0)
    weighted = jnp.concatenate([ref[...] for ref in weighted2], axis=0)
    for i, g_ref in zip(blocks, g_refs):
        hidden = jnp.concatenate([ref[i] for ref in hidden2], axis=0)
        d_both = jnp.concatenate([ref[i] for ref in d2], axis=0)
        n = d_both.shape[1]
        g_ref[:n] = mm(d_both, chosen, 0, 0).astype(g_ref.dtype)
        g_ref[n:] = mm(hidden, weighted, 0, 0).astype(g_ref.dtype)


def expand_body(my_ref, pick_ref, own_ref, out_ref, back_ref, slots_ref):
    other = jnp.concatenate([out_ref[...], back_ref[...]], axis=0)
    total = (own_ref[...] + other.astype(F32)).astype(BF16)
    slots_ref[...] = mm(place_table(my_ref[0], pick_ref), total, 1, 0).astype(BF16)


def weight_sum_body(g_own, g1, g2, g3, gate_ref, up_ref, down_ref):
    width = gate_ref.shape[0]
    for i, ref in enumerate((gate_ref, up_ref, down_ref)):
        piece = pl.ds(i * width, width)
        ref[...] = (
            g_own[piece, :].astype(F32)
            + g1[piece, :].astype(F32)
            + g2[piece, :].astype(F32)
            + g3[piece, :].astype(F32)
        ).astype(BF16)


def per_device(tokens, cotangent, pick_lists, combine, w_gate, w_up, w_down):
    n_experts = lax.axis_size("expert")
    tok_rows, feat = tokens.shape
    cap = pick_lists.shape[2]
    width = w_gate.shape[1]
    n_slots = n_experts * 2 * SLOT
    my = lax.axis_index("expert").astype(jnp.int32).reshape(1)
    sds = jax.ShapeDtypeStruct
    picks, shares = pick_lists[0], combine[0]
    slot_rows = sds((n_slots, feat), BF16)

    def exchange(rows):
        parts = rows.reshape(n_experts, 2 * SLOT, feat)
        out = lax.all_to_all(parts, "expert", split_axis=0, concat_axis=0, tiled=True)
        return out.reshape(n_slots, feat)

    hbm = pl.BlockSpec(memory_space=pl.ANY)
    send = pl.pallas_call(
        send_body,
        out_shape=slot_rows,
        in_specs=[pl.BlockSpec(memory_space=pltpu.SMEM)] + [hbm] * 4,
        out_specs=pl.BlockSpec(memory_space=pltpu.VMEM),
        scratch_shapes=[
            pltpu.VMEM(picks.shape, picks.dtype),
            pltpu.VMEM(shares.shape, shares.dtype),
            pltpu.VMEM((2 * tok_rows, feat), BF16),
            pltpu.SemaphoreType.DMA((4,)),
        ],
        cost_estimate=pl.CostEstimate(flops=3 * 10**8, bytes_accessed=2 * 10**6, transcendentals=0),
    )(my, picks, shares, tokens, cotangent)
    recv = exchange(send)
    w_own = jnp.concatenate([w_gate[0], w_up[0], w_down[0]], axis=0)
    w_all = [w_own] + [lax.ppermute(w_own, "dp", x_shift(s)) for s in (1, -1, 2)]
    block = sds((cap, feat), BF16)
    n_blocks = len(w_all)
    hidden_shape = sds((n_blocks, cap, width), BF16)
    d_shape = sds((n_blocks, cap, 2 * width), BF16)

    def swap(rows):
        return lax.ppermute(rows, "dp", HALF_SWAP)

    chosen, weighted = kernel_call(compact_body, (block,) * 2, 1, 2, 3 * 10**8, 2 * 10**6)(
        my, picks, recv
    )
    chosen_there = swap(chosen)
    weighted_there = swap(weighted)
    out_there, hidden_there, factors = kernel_call(
        forward_body,
        (block, hidden_shape, sds(d_shape.shape, F32)),
        0,
        1 + n_blocks,
        5 * 10**8,
        5 * 10**6,
    )(chosen_there, *w_all)
    out_back = swap(out_there)
    back_there, d_there = kernel_call(
        backward_body, (block, d_shape), 0, 2 + n_blocks, 5 * 10**8, 5 * 10**6
    )(weighted_there, factors, *w_all)
    back_back = swap(back_there)
    part_here, hidden_here, d_here = kernel_call(
        here_body,
        (sds((2 * cap, feat), F32), hidden_shape, d_shape),
        0,
        2 + n_blocks,
        10**9,
        6 * 10**6,
    )(chosen, weighted, *w_all)
    g_shape = (3 * width, feat)

    def grads(*refs):
        pairs = [refs[2 * i : 2 * i + 2] for i in range(4)]
        grads_body((3, 1, 2, 0), *pairs, *refs[8:])

    g_far, g_right, g_left, g_own = kernel_call(
        grads, (sds(g_shape, BF16),) * 4, 0, 8, 10**9, 6 * 10**6
    )(chosen, chosen_there, weighted, weighted_there, hidden_here, hidden_there, d_here, d_there)
    g3 = lax.ppermute(g_far, "dp", x_shift(-2))
    slots = kernel_call(expand_body, slot_rows, 1, 4, 3 * 10**8, 4 * 10**6)(
        my, picks, part_here, out_back, back_back
    )
    returned = exchange(slots)
    g1 = lax.ppermute(g_right, "dp", x_shift(-1))
    g2 = lax.ppermute(g_left, "dp", x_shift(1))
    layer_out, tokens_grad = kernel_call(
        combine_body, (sds((tok_rows, feat), BF16),) * 2, 1, 3, 4 * 10**8, 2 * 10**6
    )(my, picks, shares, returned)
    w_grads = kernel_call(
        weight_sum_body, (sds((width, feat), BF16),) * 3, 0, 4, 10**6, 5 * 10**6
    )(g_own, g1, g2, g3)
    return (layer_out, tokens_grad) + tuple(g[None] for g in w_grads)


def solution(mesh):
    rows = P(("dp", "expert"), None)
    lists = P("dp", None, None)
    weights = P("expert", "dp", None)
    return jax.shard_map(
        per_device,
        mesh=mesh,
        in_specs=(rows, rows, lists, lists, weights, weights, weights),
        out_specs=(rows, rows, weights, weights, weights),
        check_vma=False,
    )
```

```python
import jax
import jax.numpy as jnp
from jax import lax
from jax.experimental import pallas as pl
from jax.experimental.pallas import tpu as pltpu
from jax.sharding import PartitionSpec as P

N_X = 4
N_HALF = 2
SLOT = 4
BF16 = jnp.bfloat16
F32 = jnp.float32

HALF_SWAP = [(i, (i + N_X) % (N_X * N_HALF)) for i in range(N_X * N_HALF)]


def x_shift(step):
    return [
        (h * N_X + i, h * N_X + (i + step) % N_X) for h in range(N_HALF) for i in range(N_X)
    ]


def mm(a, b, contract_a, contract_b):
    return lax.dot_general(
        a, b, (((contract_a,), (contract_b,)), ((), ())), preferred_element_type=F32
    )


def kernel_call(body, out_shapes, n_smem, n_vmem, flops, nbytes):
    return pl.pallas_call(
        body,
        out_shape=out_shapes,
        in_specs=[pl.BlockSpec(memory_space=pltpu.SMEM)] * n_smem
        + [pl.BlockSpec(memory_space=pltpu.VMEM)] * n_vmem,
        out_specs=jax.tree.map(lambda _: pl.BlockSpec(memory_space=pltpu.VMEM), out_shapes),
        cost_estimate=pl.CostEstimate(flops=flops, bytes_accessed=nbytes, transcendentals=0),
        compiler_params=pltpu.CompilerParams(vmem_limit_bytes=24 * 1024 * 1024),
    )


def strictly_before(n):
    rows = lax.broadcasted_iota(jnp.int32, (n, n), 0)
    cols = lax.broadcasted_iota(jnp.int32, (n, n), 1)
    return (rows < cols).astype(BF16)


def slot_tables(my, pick, weight, tok_rows):
    n_experts, cap = pick.shape
    low = my * tok_rows
    mine = (pick >= low) & (pick < low + tok_rows)
    rank = mm(mine.astype(F32).astype(BF16), strictly_before(cap), 1, 0)
    code = jnp.where(mine, rank, -1.0)
    place = jnp.where(mine, (pick - low + 1).astype(F32), 0.0)
    shape = (n_experts, 2 * SLOT, cap)
    slot = (lax.broadcasted_iota(jnp.int32, shape, 1) % SLOT).astype(F32)
    hit = jnp.broadcast_to(code[:, None, :], shape) == slot
    row = jnp.sum(
        jnp.where(hit, jnp.broadcast_to(place[:, None, :], shape), 0.0), axis=2, keepdims=True
    )
    share = jnp.sum(
        jnp.where(hit, jnp.broadcast_to(weight[:, None, :], shape), 0.0), axis=2, keepdims=True
    )
    return row - 1.0, share


def send_body(
    my_ref, pick_hbm, weight_hbm, tok_hbm, cot_hbm, out_ref, pick_ref, weight_ref, both_ref, sems
):
    tok_rows = tok_hbm.shape[0]
    copies = [
        pltpu.make_async_copy(pick_hbm, pick_ref, sems.at[0]),
        pltpu.make_async_copy(weight_hbm, weight_ref, sems.at[1]),
        pltpu.make_async_copy(tok_hbm, both_ref.at[:tok_rows], sems.at[2]),
        pltpu.make_async_copy(cot_hbm, both_ref.at[tok_rows:], sems.at[3]),
    ]
    for copy in copies:
        copy.start()
    copies[0].wait()
    copies[1].wait()
    n_experts = pick_ref.shape[0]
    row, share = slot_tables(my_ref[0], pick_ref[...], weight_ref[...], tok_rows)
    shape = (n_experts, 2 * SLOT, 2 * tok_rows)
    lane = lax.broadcasted_iota(jnp.int32, shape, 2).astype(F32)
    second = lax.broadcasted_iota(jnp.int32, (n_experts, 2 * SLOT, 1), 1) >= SLOT
    target = jnp.where(second & (row >= 0.0), row + float(tok_rows), row)
    scale = jnp.where(second, share, 1.0)
    n_slots = n_experts * 2 * SLOT
    select = (lane == target).astype(F32).reshape(n_slots, 2 * tok_rows).astype(BF16)
    scale = jnp.broadcast_to(scale, (n_experts, 2 * SLOT, 128)).reshape(n_slots, 128)
    copies[2].wait()
    copies[3].wait()
    rows = mm(select, both_ref[...], 1, 0)
    for c in range(rows.shape[1] // 128):
        part = (rows[:, c * 128 : (c + 1) * 128] * scale).astype(BF16)
        for h in range(N_HALF):
            out_ref[h * n_slots : (h + 1) * n_slots, c * 128 : (c + 1) * 128] = part


def place_table(own, n_experts):
    cap = own.shape[1]
    n_slots = n_experts * 2 * SLOT
    source = lax.shift_right_logical(own, 7)
    from_dev = (
        lax.broadcasted_iota(jnp.int32, (n_experts, cap), 0)
        == jnp.broadcast_to(source, (n_experts, cap))
    ).astype(F32)
    rank = jnp.sum(
        from_dev * mm(from_dev.astype(BF16), strictly_before(cap), 1, 0), axis=0, keepdims=True
    )
    position = source * (2 * SLOT) + rank.astype(jnp.int32)
    both = jnp.concatenate([position, position + SLOT], axis=1)
    sub = lax.broadcasted_iota(jnp.int32, (n_slots, 2 * cap), 0)
    return (sub == jnp.broadcast_to(both, (n_slots, 2 * cap))).astype(F32).astype(BF16)


def combine_body(my_ref, pick_ref, weight_ref, slots_ref, layer_ref, grad_ref):
    n_experts = pick_ref.shape[0]
    tok_rows = layer_ref.shape[0]
    n_slots = n_experts * 2 * SLOT
    row, share = slot_tables(my_ref[0], pick_ref[...], weight_ref[...], tok_rows)
    shape = (n_experts, 2 * SLOT, tok_rows)
    lane = lax.broadcasted_iota(jnp.int32, shape, 2).astype(F32)
    second = lax.broadcasted_iota(jnp.int32, shape, 1) >= SLOT
    hit = lane == row
    high = share.astype(BF16).astype(F32)
    low = share - high
    zero = jnp.zeros(shape, F32)
    first_hit = hit & ~second
    pieces = (
        jnp.where(first_hit, high, zero),
        jnp.where(hit & second, 1.0, zero),
        jnp.where(first_hit, low, zero),
    )
    table = jnp.concatenate([p.reshape(n_slots, tok_rows).astype(BF16) for p in pieces], axis=1)
    sums = mm(table, slots_ref[:n_slots], 0, 0) + mm(table, slots_ref[n_slots:], 0, 0)
    layer_ref[...] = (sums[:tok_rows] + sums[2 * tok_rows :]).astype(BF16)
    grad_ref[...] = sums[tok_rows : 2 * tok_rows].astype(BF16)


def expert_body(
    list0_ref,
    list1_ref,
    recv_hbm,
    w0_hbm,
    w1_hbm,
    w2_hbm,
    w3_hbm,
    slots_hbm,
    saved_hbm,
    recv_ref,
    w_ref,
    slots_ref,
    saved_ref,
    recv_sems,
    w_sems,
    slot_sems,
    saved_sem,
):
    cap = list0_ref.shape[1]
    n_rows = N_HALF * cap
    n_slots = recv_ref.shape[0] // N_HALF
    n_experts = n_slots // (2 * SLOT)
    width = w_ref.shape[1] // 3
    spans = [pl.ds(h * n_slots, n_slots) for h in range(N_HALF)]
    w_copies = [
        pltpu.make_async_copy(w_hbm, w_ref.at[i], w_sems.at[i])
        for i, w_hbm in enumerate((w0_hbm, w1_hbm, w2_hbm, w3_hbm))
    ]
    recv_copies = [
        pltpu.make_async_copy(recv_hbm.at[span, :], recv_ref.at[span, :], recv_sems.at[h])
        for h, span in enumerate(spans)
    ]
    for copy in recv_copies + w_copies:
        copy.start()
    places = [place_table(ref[...], n_experts) for ref in (list0_ref, list1_ref)]
    for h, span in enumerate(spans):
        recv_copies[h].wait()
        rows = mm(places[h], recv_ref[span, :], 0, 0).astype(BF16)
        saved_ref[h * cap : (h + 1) * cap] = rows[:cap]
        saved_ref[n_rows + h * cap : n_rows + (h + 1) * cap] = rows[cap:]
    chosen, weighted = saved_ref[:n_rows], saved_ref[n_rows : 2 * n_rows]
    out = jnp.zeros(chosen.shape, F32)
    back = jnp.zeros(chosen.shape, F32)
    for i, copy in enumerate(w_copies):
        copy.wait()
        w_both, w_down = w_ref[i, : 2 * width], w_ref[i, 2 * width :]
        pre = mm(chosen, w_both, 1, 1)
        d_hidden = mm(weighted, w_down, 1, 1)
        gate, up = pre[:, :width], pre[:, width:]
        sigma = jax.nn.sigmoid(gate)
        silu = gate * sigma
        hidden = (silu * up).astype(BF16)
        d_gate = (d_hidden * up * sigma * (1.0 + gate * (1.0 - sigma))).astype(BF16)
        d_up = (d_hidden * silu).astype(BF16)
        d_both = jnp.concatenate([d_gate, d_up], axis=1)
        out = out + mm(hidden, w_down, 1, 0)
        back = back + mm(d_both, w_both, 1, 0)
        saved_ref[2 * n_rows : 3 * n_rows, i * 2 * width : (i + 1) * 2 * width] = d_both
        saved_ref[3 * n_rows :, i * width : (i + 1) * width] = hidden
    saved_ref[3 * n_rows :, len(w_copies) * width :] = jnp.zeros(
        (n_rows, saved_ref.shape[1] - len(w_copies) * width), BF16
    )
    copies = [pltpu.make_async_copy(saved_ref, saved_hbm, saved_sem.at[0])]
    for h, span in enumerate(spans):
        total = jnp.concatenate(
            [out[h * cap : (h + 1) * cap], back[h * cap : (h + 1) * cap]], axis=0
        ).astype(BF16)
        slots_ref[span, :] = mm(places[h], total, 1, 0).astype(BF16)
        copy = pltpu.make_async_copy(
            slots_ref.at[span, :], slots_hbm.at[span, :], slot_sems.at[h]
        )
        copy.start()
        copies.append(copy)
    copies[0].start()
    for copy in copies:
        copy.wait()


def grads_body(saved_ref, *g_refs):
    n_rows = saved_ref.shape[0] // 4
    width = g_refs[0].shape[0] // 3
    chosen, weighted = saved_ref[:n_rows], saved_ref[n_rows : 2 * n_rows]
    for i, g_ref in enumerate(g_refs):
        d_both = saved_ref[2 * n_rows : 3 * n_rows, i * 2 * width : (i + 1) * 2 * width]
        hidden = saved_ref[3 * n_rows :, i * width : (i + 1) * width]
        g_ref[: 2 * width] = mm(d_both, chosen, 0, 0).astype(BF16)
        g_ref[2 * width :] = mm(hidden, weighted, 0, 0).astype(BF16)


def weight_sum_body(g_own, g1, g2, g3, gate_ref, up_ref, down_ref):
    width = gate_ref.shape[0]
    for i, ref in enumerate((gate_ref, up_ref, down_ref)):
        piece = pl.ds(i * width, width)
        ref[...] = (
            g_own[piece, :].astype(F32)
            + g1[piece, :].astype(F32)
            + g2[piece, :].astype(F32)
            + g3[piece, :].astype(F32)
        ).astype(BF16)


def per_device(tokens, cotangent, pick_lists, combine, w_gate, w_up, w_down):
    n_experts = lax.axis_size("expert")
    tok_rows, feat = tokens.shape
    cap = pick_lists.shape[2]
    width = w_gate.shape[1]
    n_peers = N_HALF * n_experts
    n_slots = n_peers * 2 * SLOT
    my = lax.axis_index("expert").astype(jnp.int32).reshape(1)
    half = lax.axis_index("dp") // N_X
    sds = jax.ShapeDtypeStruct
    picks, shares = pick_lists[0], combine[0]
    slot_rows = sds((n_slots, feat), BF16)
    groups = [
        [(h * N_X + x) * n_experts + e for h in range(N_HALF) for e in range(n_experts)]
        for x in range(N_X)
    ]

    def exchange(rows):
        out = lax.all_to_all(
            rows.reshape(n_peers, 2 * SLOT, feat),
            ("dp", "expert"),
            split_axis=0,
            concat_axis=0,
            axis_index_groups=groups,
            tiled=True,
        )
        return out.reshape(n_slots, feat)

    hbm = pl.BlockSpec(memory_space=pl.ANY)
    send = pl.pallas_call(
        send_body,
        out_shape=slot_rows,
        in_specs=[pl.BlockSpec(memory_space=pltpu.SMEM)] + [hbm] * 4,
        out_specs=pl.BlockSpec(memory_space=pltpu.VMEM),
        scratch_shapes=[
            pltpu.VMEM(picks.shape, picks.dtype),
            pltpu.VMEM(shares.shape, shares.dtype),
            pltpu.VMEM((2 * tok_rows, feat), BF16),
            pltpu.SemaphoreType.DMA((4,)),
        ],
        cost_estimate=pl.CostEstimate(flops=3 * 10**8, bytes_accessed=3 * 10**6, transcendentals=0),
    )(my, picks, shares, tokens, cotangent)
    recv = exchange(send)
    w_own = jnp.concatenate([w_gate[0], w_up[0], w_down[0]], axis=0)
    w_all = [w_own] + [lax.ppermute(w_own, "dp", x_shift(s)) for s in (1, -1, 2)]
    list_here = lax.dynamic_slice_in_dim(picks, my[0], 1, 0)
    list_there = lax.ppermute(list_here, "dp", HALF_SWAP)
    lists = [jnp.where(half == h, list_here, list_there) for h in range(N_HALF)]
    n_rows = N_HALF * cap
    n_blocks = len(w_all)
    saved_rows = sds((4 * n_rows, feat), BF16)
    vmem = pl.BlockSpec(memory_space=pltpu.VMEM)
    slots, saved = pl.pallas_call(
        expert_body,
        out_shape=(slot_rows, saved_rows),
        in_specs=[vmem] * N_HALF + [hbm] * (1 + n_blocks),
        out_specs=(hbm, hbm),
        scratch_shapes=[
            pltpu.VMEM(slot_rows.shape, BF16),
            pltpu.VMEM((n_blocks, 3 * width, feat), BF16),
            pltpu.VMEM(slot_rows.shape, BF16),
            pltpu.VMEM(saved_rows.shape, BF16),
        ]
        + [pltpu.SemaphoreType.DMA((n,)) for n in (N_HALF, n_blocks, N_HALF, 1)],
        cost_estimate=pl.CostEstimate(
            flops=3 * 10**9, bytes_accessed=10**7, transcendentals=0
        ),
        compiler_params=pltpu.CompilerParams(vmem_limit_bytes=62 * 1024 * 1024),
    )(*lists, recv, *w_all)
    returned = exchange(slots)
    g_own, *g_others = kernel_call(
        grads_body, (sds((3 * width, feat), BF16),) * n_blocks, 0, 1, 2 * 10**9, 5 * 10**6
    )(saved)
    g_home = [lax.ppermute(g, "dp", x_shift(-s)) for g, s in zip(g_others, (1, -1, 2))]
    layer_out, tokens_grad = kernel_call(
        combine_body, (sds((tok_rows, feat), BF16),) * 2, 1, 3, 8 * 10**8, 3 * 10**6
    )(my, picks, shares, returned)
    w_grads = kernel_call(
        weight_sum_body, (sds((width, feat), BF16),) * 3, 0, 4, 10**6, 5 * 10**6
    )(g_own, *g_home)
    return (layer_out, tokens_grad) + tuple(g[None] for g in w_grads)


def solution(mesh):
    rows = P(("dp", "expert"), None)
    lists = P("dp", None, None)
    weights = P("expert", "dp", None)
    return jax.shard_map(
        per_device,
        mesh=mesh,
        in_specs=(rows, rows, lists, lists, weights, weights, weights),
        out_specs=(rows, rows, weights, weights, weights),
        check_vma=False,
    )
```

```python
import jax
import jax.numpy as jnp
from jax import lax
from jax.experimental import pallas as pl
from jax.experimental.pallas import tpu as pltpu
from jax.sharding import PartitionSpec as P

N_X = 4
N_HALF = 2
SLOT = 4
BF16 = jnp.bfloat16
F32 = jnp.float32

HALF_SWAP = [(i, (i + N_X) % (N_X * N_HALF)) for i in range(N_X * N_HALF)]


def x_shift(step):
    return [
        (h * N_X + i, h * N_X + (i + step) % N_X) for h in range(N_HALF) for i in range(N_X)
    ]


def mm(a, b, contract_a, contract_b):
    return lax.dot_general(
        a, b, (((contract_a,), (contract_b,)), ((), ())), preferred_element_type=F32
    )


SMALL = pltpu.CompilerParams(vmem_limit_bytes=24 * 1024 * 1024)


def kernel_call(body, out_shapes, n_smem, n_vmem, flops, nbytes):
    return pl.pallas_call(
        body,
        out_shape=out_shapes,
        in_specs=[pl.BlockSpec(memory_space=pltpu.SMEM)] * n_smem
        + [pl.BlockSpec(memory_space=pltpu.VMEM)] * n_vmem,
        out_specs=jax.tree.map(lambda _: pl.BlockSpec(memory_space=pltpu.VMEM), out_shapes),
        cost_estimate=pl.CostEstimate(flops=flops, bytes_accessed=nbytes, transcendentals=0),
        compiler_params=SMALL,
    )


def strictly_before(n):
    rows = lax.broadcasted_iota(jnp.int32, (n, n), 0)
    cols = lax.broadcasted_iota(jnp.int32, (n, n), 1)
    return (rows < cols).astype(BF16)


def slot_tables(my, pick, weight, tok_rows):
    n_experts, cap = pick.shape
    low = my * tok_rows
    mine = (pick >= low) & (pick < low + tok_rows)
    rank = mm(mine.astype(F32).astype(BF16), strictly_before(cap), 1, 0)
    code = jnp.where(mine, rank, -1.0)
    place = jnp.where(mine, (pick - low + 1).astype(F32), 0.0)
    shape = (n_experts, 2 * SLOT, cap)
    slot = (lax.broadcasted_iota(jnp.int32, shape, 1) % SLOT).astype(F32)
    hit = jnp.broadcast_to(code[:, None, :], shape) == slot
    row = jnp.sum(
        jnp.where(hit, jnp.broadcast_to(place[:, None, :], shape), 0.0), axis=2, keepdims=True
    )
    share = jnp.sum(
        jnp.where(hit, jnp.broadcast_to(weight[:, None, :], shape), 0.0), axis=2, keepdims=True
    )
    return row - 1.0, share


def stream_out(buffer, hbm, sems, piece):
    n = sems.shape[0]
    rows = buffer.shape[0] // n
    copies = []
    for c in range(n):
        span = pl.ds(c * rows, rows)
        buffer[span, :] = piece(c * rows, rows)
        copies.append(pltpu.make_async_copy(buffer.at[span, :], hbm.at[span, :], sems.at[c]))
        copies[-1].start()
    for copy in copies:
        copy.wait()


def send_body(
    my_ref,
    pick_hbm,
    weight_hbm,
    tok_hbm,
    cot_hbm,
    out_hbm,
    pick_ref,
    weight_ref,
    both_ref,
    out_ref,
    sems,
    out_sems,
):
    tok_rows = tok_hbm.shape[0]
    copies = [
        pltpu.make_async_copy(pick_hbm, pick_ref, sems.at[0]),
        pltpu.make_async_copy(weight_hbm, weight_ref, sems.at[1]),
        pltpu.make_async_copy(tok_hbm, both_ref.at[:tok_rows], sems.at[2]),
        pltpu.make_async_copy(cot_hbm, both_ref.at[tok_rows:], sems.at[3]),
    ]
    for copy in copies:
        copy.start()
    copies[0].wait()
    copies[1].wait()
    n_experts = pick_ref.shape[0]
    row, share = slot_tables(my_ref[0], pick_ref[...], weight_ref[...], tok_rows)
    shape = (n_experts, 2 * SLOT, 2 * tok_rows)
    lane = lax.broadcasted_iota(jnp.int32, shape, 2).astype(F32)
    second = lax.broadcasted_iota(jnp.int32, (n_experts, 2 * SLOT, 1), 1) >= SLOT
    target = jnp.where(second & (row >= 0.0), row + float(tok_rows), row)
    scale = jnp.where(second, share, 1.0)
    n_slots = n_experts * 2 * SLOT
    select = (lane == target).astype(F32).reshape(n_slots, 2 * tok_rows).astype(BF16)
    scale = jnp.broadcast_to(scale, (n_experts, 2 * SLOT, 128)).reshape(n_slots, 128)
    copies[2].wait()
    copies[3].wait()

    def piece(start, n):
        rows = mm(select[start : start + n], both_ref[...], 1, 0)
        factor = scale[start : start + n]
        return jnp.concatenate(
            [rows[:, c : c + 128] * factor for c in range(0, rows.shape[1], 128)], axis=1
        ).astype(BF16)

    stream_out(out_ref, out_hbm, out_sems, piece)


def place_table(my, pick_ref):
    n_experts, cap = pick_ref.shape
    n_slots = n_experts * 2 * SLOT
    own = pick_ref[pl.ds(my, 1), :]
    source = lax.shift_right_logical(own, 7)
    from_dev = (
        lax.broadcasted_iota(jnp.int32, (n_experts, cap), 0)
        == jnp.broadcast_to(source, (n_experts, cap))
    ).astype(F32)
    rank = jnp.sum(
        from_dev * mm(from_dev.astype(BF16), strictly_before(cap), 1, 0), axis=0, keepdims=True
    )
    position = source * (2 * SLOT) + rank.astype(jnp.int32)
    both = jnp.concatenate([position, position + SLOT], axis=1)
    sub = lax.broadcasted_iota(jnp.int32, (n_slots, 2 * cap), 0)
    return (sub == jnp.broadcast_to(both, (n_slots, 2 * cap))).astype(F32).astype(BF16)


def combine_body(my_ref, pick_ref, weight_ref, slots_ref, layer_ref, grad_ref):
    n_experts = pick_ref.shape[0]
    tok_rows = layer_ref.shape[0]
    n_slots = n_experts * 2 * SLOT
    row, share = slot_tables(my_ref[0], pick_ref[...], weight_ref[...], tok_rows)
    shape = (n_experts, 2 * SLOT, tok_rows)
    lane = lax.broadcasted_iota(jnp.int32, shape, 2).astype(F32)
    second = lax.broadcasted_iota(jnp.int32, shape, 1) >= SLOT
    hit = lane == row
    high = share.astype(BF16).astype(F32)
    low = share - high
    zero = jnp.zeros(shape, F32)
    first_hit = hit & ~second
    pieces = (
        jnp.where(first_hit, high, zero),
        jnp.where(hit & second, 1.0, zero),
        jnp.where(first_hit, low, zero),
    )
    table = jnp.concatenate([p.reshape(n_slots, tok_rows).astype(BF16) for p in pieces], axis=1)
    sums = mm(table, slots_ref[...], 0, 0)
    layer_ref[...] = (sums[:tok_rows] + sums[2 * tok_rows :]).astype(BF16)
    grad_ref[...] = sums[tok_rows : 2 * tok_rows].astype(BF16)


def compact_body(my_ref, pick_ref, recv_hbm, chosen_ref, weighted_ref, recv_ref, sems):
    n = sems.shape[0]
    n_rows = recv_ref.shape[0] // n
    spans = [pl.ds(c * n_rows, n_rows) for c in range(n)]
    copies = [
        pltpu.make_async_copy(recv_hbm.at[span, :], recv_ref.at[span, :], sems.at[c])
        for c, span in enumerate(spans)
    ]
    for copy in copies:
        copy.start()
    place = place_table(my_ref[0], pick_ref)
    rows = jnp.zeros((place.shape[1], recv_ref.shape[1]), F32)
    for c, copy in enumerate(copies):
        copy.wait()
        rows = rows + mm(place[c * n_rows : (c + 1) * n_rows], recv_ref[spans[c], :], 0, 0)
    rows = rows.astype(BF16)
    cap = chosen_ref.shape[0]
    chosen_ref[...] = rows[:cap]
    weighted_ref[...] = rows[cap:]


def forward(chosen, w_ref):
    width = w_ref.shape[0] // 3
    pre = mm(chosen, w_ref[: 2 * width], 1, 1)
    gate, up = pre[:, :width], pre[:, width:]
    sigma = jax.nn.sigmoid(gate)
    silu = gate * sigma
    slope = up * sigma * (1.0 + gate * (1.0 - sigma))
    return (silu * up).astype(BF16), slope, silu


def backward(weighted, slope, silu, w_ref):
    d_hidden = mm(weighted, w_ref[2 * (w_ref.shape[0] // 3) :], 1, 1)
    return jnp.concatenate([(d_hidden * slope).astype(BF16), (d_hidden * silu).astype(BF16)], axis=1)


def forward_body(chosen_ref, w0, w1, w2, w3, out_ref, hidden_ref, factor_ref):
    width = w0.shape[0] // 3
    chosen = chosen_ref[...]
    out = jnp.zeros(chosen.shape, F32)
    for i, w_ref in enumerate((w0, w1, w2, w3)):
        hidden, slope, silu = forward(chosen, w_ref)
        out = out + mm(hidden, w_ref[2 * width :], 1, 0)
        hidden_ref[i] = hidden
        factor_ref[i, :, :width] = slope
        factor_ref[i, :, width:] = silu
    out_ref[...] = out.astype(BF16)


def backward_body(weighted_ref, factor_ref, w0, w1, w2, w3, back_ref, d_ref):
    width = w0.shape[0] // 3
    weighted = weighted_ref[...]
    back = jnp.zeros(weighted.shape, F32)
    for i, w_ref in enumerate((w0, w1, w2, w3)):
        d_both = backward(weighted, factor_ref[i, :, :width], factor_ref[i, :, width:], w_ref)
        back = back + mm(d_both, w_ref[: 2 * width], 1, 0)
        d_ref[i] = d_both
    back_ref[...] = back.astype(BF16)


def here_body(chosen_ref, weighted_ref, w0, w1, w2, w3, part_ref, hidden_ref, d_ref):
    width = w0.shape[0] // 3
    chosen, weighted = chosen_ref[...], weighted_ref[...]
    cap = chosen.shape[0]
    out = jnp.zeros(chosen.shape, F32)
    back = jnp.zeros(chosen.shape, F32)
    for i, w_ref in enumerate((w0, w1, w2, w3)):
        hidden, slope, silu = forward(chosen, w_ref)
        d_both = backward(weighted, slope, silu, w_ref)
        out = out + mm(hidden, w_ref[2 * width :], 1, 0)
        back = back + mm(d_both, w_ref[: 2 * width], 1, 0)
        hidden_ref[i] = hidden
        d_ref[i] = d_both
    part_ref[:cap] = out
    part_ref[cap:] = back


def grads_body(blocks, chosen2, weighted2, hidden2, d2, *g_refs):
    chosen = jnp.concatenate([ref[...] for ref in chosen2], axis=0)
    weighted = jnp.concatenate([ref[...] for ref in weighted2], axis=0)
    for i, g_ref in zip(blocks, g_refs):
        hidden = jnp.concatenate([ref[i] for ref in hidden2], axis=0)
        d_both = jnp.concatenate([ref[i] for ref in d2], axis=0)
        n = d_both.shape[1]
        g_ref[:n] = mm(d_both, chosen, 0, 0).astype(g_ref.dtype)
        g_ref[n:] = mm(hidden, weighted, 0, 0).astype(g_ref.dtype)


def expand_body(my_ref, pick_ref, own_ref, out_ref, back_ref, slots_hbm, slots_ref, sems):
    other = jnp.concatenate([out_ref[...], back_ref[...]], axis=0)
    total = (own_ref[...] + other.astype(F32)).astype(BF16)
    place = place_table(my_ref[0], pick_ref)

    def piece(start, n):
        return mm(place[start : start + n], total, 1, 0).astype(BF16)

    stream_out(slots_ref, slots_hbm, sems, piece)


def weight_sum_body(g_own, g1, g2, g3, gate_ref, up_ref, down_ref):
    width = gate_ref.shape[0]
    for i, ref in enumerate((gate_ref, up_ref, down_ref)):
        piece = pl.ds(i * width, width)
        ref[...] = (
            g_own[piece, :].astype(F32)
            + g1[piece, :].astype(F32)
            + g2[piece, :].astype(F32)
            + g3[piece, :].astype(F32)
        ).astype(BF16)


def per_device(tokens, cotangent, pick_lists, combine, w_gate, w_up, w_down):
    n_experts = lax.axis_size("expert")
    tok_rows, feat = tokens.shape
    cap = pick_lists.shape[2]
    width = w_gate.shape[1]
    n_slots = n_experts * 2 * SLOT
    my = lax.axis_index("expert").astype(jnp.int32).reshape(1)
    sds = jax.ShapeDtypeStruct
    picks, shares = pick_lists[0], combine[0]
    slot_rows = sds((n_slots, feat), BF16)

    def exchange(rows):
        parts = rows.reshape(n_experts, 2 * SLOT, feat)
        out = lax.all_to_all(parts, "expert", split_axis=0, concat_axis=0, tiled=True)
        return out.reshape(n_slots, feat)

    smem = pl.BlockSpec(memory_space=pltpu.SMEM)
    vmem = pl.BlockSpec(memory_space=pltpu.VMEM)
    hbm = pl.BlockSpec(memory_space=pl.ANY)
    dma = pltpu.SemaphoreType.DMA
    slot_buffer = pltpu.VMEM(slot_rows.shape, slot_rows.dtype)
    send = pl.pallas_call(
        send_body,
        out_shape=slot_rows,
        in_specs=[smem] + [hbm] * 4,
        out_specs=hbm,
        scratch_shapes=[
            pltpu.VMEM(picks.shape, picks.dtype),
            pltpu.VMEM(shares.shape, shares.dtype),
            pltpu.VMEM((2 * tok_rows, feat), BF16),
            slot_buffer,
            dma((4,)),
            dma((4,)),
        ],
        cost_estimate=pl.CostEstimate(flops=3 * 10**8, bytes_accessed=2 * 10**6, transcendentals=0),
    )(my, picks, shares, tokens, cotangent)
    recv = exchange(send)
    w_own = jnp.concatenate([w_gate[0], w_up[0], w_down[0]], axis=0)
    w_all = [w_own] + [lax.ppermute(w_own, "dp", x_shift(s)) for s in (1, -1, 2)]
    block = sds((cap, feat), BF16)
    n_blocks = len(w_all)
    hidden_shape = sds((n_blocks, cap, width), BF16)
    d_shape = sds((n_blocks, cap, 2 * width), BF16)

    def swap(rows):
        return lax.ppermute(rows, "dp", HALF_SWAP)

    chosen, weighted = pl.pallas_call(
        compact_body,
        out_shape=(block, block),
        in_specs=[smem, vmem, hbm],
        out_specs=(vmem, vmem),
        scratch_shapes=[slot_buffer, dma((4,))],
        cost_estimate=pl.CostEstimate(flops=3 * 10**8, bytes_accessed=2 * 10**6, transcendentals=0),
        compiler_params=SMALL,
    )(my, picks, recv)
    chosen_there = swap(chosen)
    weighted_there = swap(weighted)
    out_there, hidden_there, factors = kernel_call(
        forward_body,
        (block, hidden_shape, sds(d_shape.shape, F32)),
        0,
        1 + n_blocks,
        5 * 10**8,
        5 * 10**6,
    )(chosen_there, *w_all)
    out_back = swap(out_there)
    back_there, d_there = kernel_call(
        backward_body, (block, d_shape), 0, 2 + n_blocks, 5 * 10**8, 5 * 10**6
    )(weighted_there, factors, *w_all)
    back_back = swap(back_there)
    part_here, hidden_here, d_here = kernel_call(
        here_body,
        (sds((2 * cap, feat), F32), hidden_shape, d_shape),
        0,
        2 + n_blocks,
        10**9,
        6 * 10**6,
    )(chosen, weighted, *w_all)
    g_shape = (3 * width, feat)

    def grads(*refs):
        pairs = [refs[2 * i : 2 * i + 2] for i in range(4)]
        grads_body((3, 1, 2, 0), *pairs, *refs[8:])

    g_far, g_right, g_left, g_own = kernel_call(
        grads, (sds(g_shape, BF16),) * 4, 0, 8, 10**9, 6 * 10**6
    )(chosen, chosen_there, weighted, weighted_there, hidden_here, hidden_there, d_here, d_there)
    g3 = lax.ppermute(g_far, "dp", x_shift(-2))
    g1 = lax.ppermute(g_right, "dp", x_shift(-1))
    g2 = lax.ppermute(g_left, "dp", x_shift(1))
    slots = pl.pallas_call(
        expand_body,
        out_shape=slot_rows,
        in_specs=[smem] + [vmem] * 4,
        out_specs=hbm,
        scratch_shapes=[slot_buffer, dma((4,))],
        cost_estimate=pl.CostEstimate(flops=3 * 10**8, bytes_accessed=4 * 10**6, transcendentals=0),
        compiler_params=SMALL,
    )(my, picks, part_here, out_back, back_back)
    returned = exchange(slots)
    layer_out, tokens_grad = kernel_call(
        combine_body, (sds((tok_rows, feat), BF16),) * 2, 1, 3, 4 * 10**8, 2 * 10**6
    )(my, picks, shares, returned)
    w_grads = kernel_call(
        weight_sum_body, (sds((width, feat), BF16),) * 3, 0, 4, 10**6, 5 * 10**6
    )(g_own, g1, g2, g3)
    return (layer_out, tokens_grad) + tuple(g[None] for g in w_grads)


def solution(mesh):
    rows = P(("dp", "expert"), None)
    lists = P("dp", None, None)
    weights = P("expert", "dp", None)
    return jax.shard_map(
        per_device,
        mesh=mesh,
        in_specs=(rows, rows, lists, lists, weights, weights, weights),
        out_specs=(rows, rows, weights, weights, weights),
        check_vma=False,
    )
```
